512 devices in a mesh: expert: 8 (over y), tensor: 64 (over z, x, core).
Axes of the slice: x: 4, y: 8, z: 8, core: 2. Of those that a mesh axis runs over, the one named last changes fastest.
Arguments:
- expert_hidden: bfloat16 [8, 768, 8192], P('expert', 'tensor'), may hold values from -6 to 6
- probe_tangent: bfloat16 [8, 6144, 8192], P('expert', 'tensor'), may hold values from -0.0625 to 0.0625
- routed_experts: int32 [1536, 2], P('expert'), may hold values from 0 to 7, all different within a row; in each aligned block of 192 rows (0 to 191, 192 to 383, ...) at most 96 rows name the same one
- gate_weights: float32 [1536, 2], P('expert'), may hold values from 0.1 to 1
Outputs:
- ggn_product: bfloat16 [8, 6144, 8192], P('expert', 'tensor')
- token_quadratic: float32 [1536], P('expert')
The draws below stay inside these ranges and needn't reach their ends.
Inputs may be any that keep to these rules, and one draw needn't show every extreme that they name: `routed_experts`: each row names two different experts. Among the 192 rows of one source, no expert is named by more than 96 rows, a bound that some block reaches.
All inputs are finite; a program needn't handle non-finite values.
Results may differ from the reference program's by a relative error of at most 0.0057.
Values may be sent and summed in bfloat16 or wider, within the bound.
No kernel may reach another device: no remote copies, remote signals or barrier semaphores. Data moves between devices by JAX's collectives and lax.ppermute only.
A program may use at most 128 MiB of HBM per device.

```python
import math
import jax
import jax.numpy as jnp
import numpy as np
from jax import lax

D = 6144
FF = 8192
TOK_DEV = 192
EXPERTS = 8
CAP = 96
ROWS = 768
TOKENS = 1536
N_EXPERT = 8


def block_scale(own_key, extent, split, smallest, top_value):
    def one(dim, parts):
        draws = jax.random.uniform(jax.random.fold_in(jax.random.fold_in(own_key, 6), dim), (parts,), jnp.float32, smallest / len(split), top_value / len(split))
        return jnp.repeat(jnp.exp(draws), extent[dim] // parts).reshape((-1,) + (1,) * (len(extent) - dim - 1))

    loudness = one(*split[0])
    for cut in split[1:]:
        loudness = loudness * one(*cut)
    return loudness


def deal_out(key, own, number, rows, number_of, top, most, lean):
    ranking = jax.random.permutation(key, number_of)
    crowded, ordinary = load_shares(number_of, rows * top, most, lean, True), load_shares(number_of, rows * top, most, lean, False)
    places = jnp.arange(number_of)

    def named(lengths, turn):
        used = int((lengths > 0).sum())
        fixed = max(1, used // 4)
        moved = fixed + (places - fixed + turn * (used - fixed)) % max(1, number_of - fixed)
        return jnp.zeros((number_of,), jnp.int32).at[ranking[jnp.where(places < fixed, places, moved)]].set(jnp.asarray(lengths, jnp.int32))

    lengths = jnp.where(number % 4 == 0, named(crowded, number // 4), named(ordinary, number - number // 4 - 1))
    mixed = jax.random.permutation(jax.random.fold_in(own, 3), number_of)
    donor, receiver = mixed[0:number_of // 2 * 2:2], mixed[1:number_of // 2 * 2:2]
    margin = jnp.minimum(lengths[donor] - 1, most - lengths[receiver]) // 2
    margin = jnp.where((donor == ranking[0]) | (receiver == ranking[0]) | (lengths[receiver] == 0), 0, jnp.maximum(margin, 0))
    moved = jax.random.randint(jax.random.fold_in(own, 4), (number_of // 2,), 0, 1 << 20) % (margin + 1)
    lengths = lengths.at[donor].add(-moved).at[receiver].add(moved)
    members = jnp.searchsorted(jnp.cumsum(lengths), jnp.arange(rows * top), side="right").astype(jnp.int32)
    table = members.reshape(top, rows).T
    table = table[jax.random.permutation(jax.random.fold_in(own, 1), rows)]
    turn = jax.random.randint(jax.random.fold_in(own, 2), (rows, 1), 0, top)
    return jnp.take_along_axis(table, (jnp.arange(top)[None, :] + turn) % top, axis=1)


def load_shares(count, total, most, lean, full):
    weights = [(1 << 20) // math.isqrt(rank ** lean) + 1 for rank in range(1, count + 1)]
    largest = most if full else min(most, max(-(-total // count), total * weights[0] // sum(weights)))
    least = 1 if total - largest >= count - 1 else 0
    counts, rest = [largest] + [least] * (count - 1), total - largest - least * (count - 1)
    while rest > 0:
        candidates = [i for i in range(1, count) if counts[i] < largest] or [i for i in range(1, count) if counts[i] < most]
        pool, remaining = sum([weights[i] for i in candidates]), rest
        for i in candidates:
            extra = min(most - counts[i], max(1, remaining * weights[i] // pool), rest)
            counts[i] = counts[i] + extra
            rest = rest - extra
    return np.array(counts)


def scatter_about(rng, dims, width, bound, pieces=(), kind=jnp.bfloat16):
    entries = jax.random.normal(rng, dims, jnp.float32) * width
    if len(pieces) > 0:
        entries = block_scale(rng, dims, pieces, -0.22, 0.18) * entries
    return jnp.clip(entries, min=-bound, max=bound).astype(kind)


def setup_inputs(seed: int = 0) -> dict:
    streams_of = jax.random.split(jax.random.key(seed), 5)
    expert_hidden = scatter_about(streams_of[0], (EXPERTS, ROWS, FF), 1.0, 6.0, ((0, 8), (1, 64)))
    probe_tangent = scatter_about(streams_of[1], (EXPERTS, D, FF), FF ** -0.5, 0.0625, ((0, 8), (1, 64)))
    routed_experts_keys = jax.random.split(jax.random.fold_in(streams_of[2], 1), TOKENS // TOK_DEV)
    routed_experts_turns = jax.random.permutation(jax.random.fold_in(streams_of[2], 3), TOKENS // TOK_DEV)
    routed_experts = jax.vmap(lambda own, number: deal_out(jax.random.fold_in(streams_of[2], 2), own, number, TOK_DEV, EXPERTS, 2, CAP, 2))(routed_experts_keys, routed_experts_turns).reshape((TOKENS, 2))
    gate_weights = jnp.clip(0.1 + 0.9 * jax.random.uniform(streams_of[3], (TOKENS, 2), jnp.float32) ** block_scale(streams_of[3], (TOKENS, 2), ((0, 8),), -0.2, 0.2), 0.1, 1.0)
    return dict(expert_hidden=expert_hidden, probe_tangent=probe_tangent, routed_experts=routed_experts, gate_weights=gate_weights)


def expert_forward(operands):
    hidden_rows, probe_rows = operands
    return jnp.dot(hidden_rows, probe_rows.T, preferred_element_type=jnp.float32).astype(jnp.bfloat16)


def expert_backward(operands):
    returned_rows, hidden_rows = operands
    return jnp.dot(returned_rows.T, hidden_rows, preferred_element_type=jnp.float32).astype(jnp.bfloat16)


def reference(expert_hidden, probe_tangent, routed_experts, gate_weights):
    pair_count = TOK_DEV * 2
    source_ids = routed_experts.reshape(N_EXPERT, pair_count).astype(jnp.int32)
    expert_range = jnp.arange(N_EXPERT, dtype=jnp.int32)
    one_hot = (source_ids[:, :, None] == expert_range[None, None, :]).astype(jnp.int32)
    earlier = (jnp.cumsum(one_hot, axis=1).astype(jnp.int32) - one_hot).astype(jnp.int32)
    slot_rank = jnp.sum(one_hot * earlier, axis=2).astype(jnp.int32)
    buffer_row = (jnp.arange(N_EXPERT, dtype=jnp.int32)[:, None] * CAP + slot_rank).astype(jnp.int32)
    expert_flat = source_ids.reshape(-1)
    row_flat = buffer_row.reshape(-1)
    gate_flat = gate_weights.reshape(-1)

    expert_tangent = lax.map(expert_forward, (expert_hidden, probe_tangent))
    picked = expert_tangent[expert_flat, row_flat].astype(jnp.float32) * gate_flat[:, None]
    token_tangent = jnp.sum(picked.reshape(TOKENS, 2, D), axis=1)
    token_quadratic = jnp.sum(token_tangent * token_tangent, axis=1) / D

    weighted = (token_tangent[:, None, :] * gate_weights[:, :, None]).reshape(TOKENS * 2, D).astype(jnp.bfloat16)
    returned = jnp.zeros((N_EXPERT, ROWS, D), jnp.bfloat16).at[expert_flat, row_flat].set(weighted)
    ggn_product = lax.map(expert_backward, (returned, expert_hidden))
    return ggn_product, token_quadratic
```

```python
import jax
import jax.numpy as jnp
from jax import lax
from jax.experimental import pallas as pl
from jax.experimental.pallas import tpu as pltpu
from jax.sharding import Mesh, PartitionSpec as P


LANES = 128


def forward_kernel(x_ref, p_ref, o_ref, pc_ref, y0_ref, y1_ref):
    cols, half = p_ref.shape[0], x_ref.shape[1]
    rows = o_ref.shape[0]

    @pl.when(pl.program_id(0) == 0)
    def _():
        pc_ref[...] = jnp.zeros_like(pc_ref)
        pc_ref[0:cols, :] = p_ref[:, 0:half]
        pc_ref[LANES : LANES + cols, :] = p_ref[:, half : 2 * half]

    y = lax.dot_general(
        x_ref[...], pc_ref[...], (((1,), (1,)), ((), ())), preferred_element_type=jnp.float32
    )
    y0_ref[...] = y[:, 0:LANES]
    y1_ref[...] = y[:, LANES : 2 * LANES]
    total = y0_ref[pl.ds(0, rows, stride=2), :] + y1_ref[pl.ds(1, rows, stride=2), :]
    o_ref[...] = total.astype(o_ref.dtype)


def forward(x, probe, block=384):
    rows, half = x.shape
    cols = probe.shape[0]
    return pl.pallas_call(
        forward_kernel,
        grid=(rows // block,),
        in_specs=[
            pl.BlockSpec((block, half), lambda i: (i, 0)),
            pl.BlockSpec((cols, 2 * half), lambda i: (0, 0)),
        ],
        out_specs=pl.BlockSpec((block // 2, LANES), lambda i: (i, 0)),
        out_shape=jax.ShapeDtypeStruct((rows // 2, LANES), jnp.bfloat16),
        scratch_shapes=[
            pltpu.VMEM((2 * LANES, half), jnp.bfloat16),
            pltpu.VMEM((block, LANES), jnp.float32),
            pltpu.VMEM((block, LANES), jnp.float32),
        ],
    )(x, probe)


def combine_kernel(t_ref, row_ref, gate_ref, b_ref, q_ref):
    rows = t_ref.shape[0]
    toks = row_ref.shape[0]
    lane = lax.broadcasted_iota(jnp.int32, (toks, rows), 1)
    zero = jnp.zeros((toks, rows), jnp.bfloat16)
    one = jnp.ones((toks, rows), jnp.bfloat16)
    total = None
    picks = []
    for k in range(2):
        pick = jnp.where(lane == row_ref[:, k : k + 1], one, zero)
        part = jnp.dot(pick, t_ref[...], preferred_element_type=jnp.float32)
        part = part * gate_ref[:, k : k + 1]
        total = part if total is None else total + part
        picks.append(pick)
    back = None
    for k in range(2):
        weighted = (total * gate_ref[:, k : k + 1]).astype(jnp.bfloat16)
        placed = lax.dot_general(
            picks[k], weighted, (((0,), (0,)), ((), ())), preferred_element_type=jnp.float32
        )
        back = placed if back is None else back + placed
    b_ref[...] = back.astype(b_ref.dtype)
    squares = jnp.sum(total * total, axis=1, keepdims=True)
    q_ref[...] = jnp.broadcast_to(squares, (toks, LANES)).T[0:8]


def combine(tangent, row, gate):
    rows = tangent.shape[0]
    toks = row.shape[0]
    return pl.pallas_call(
        combine_kernel,
        out_shape=(
            jax.ShapeDtypeStruct((rows, LANES), jnp.bfloat16),
            jax.ShapeDtypeStruct((8, toks), jnp.float32),
        ),
    )(tangent, row, gate)


def backward_kernel(r_ref, x_ref, o_ref, e_ref, f_ref, rt_ref, g_ref, sem):
    cols, half = o_ref.shape[0], o_ref.shape[1] // 2
    rows = r_ref.shape[0]
    block = x_ref.shape[1]
    step = pl.program_id(0)
    steps = pl.num_programs(0)

    @pl.when(step == 0)
    def _():
        rf = r_ref[...].astype(jnp.float32)
        zero = jnp.zeros_like(rf)
        e_ref[pl.ds(0, rows, stride=2), :] = rf
        e_ref[pl.ds(1, rows, stride=2), :] = zero
        f_ref[pl.ds(0, rows, stride=2), :] = zero
        f_ref[pl.ds(1, rows, stride=2), :] = rf
        rt_ref[0:cols, :] = e_ref[...].T.astype(jnp.bfloat16)[0:cols]
        rt_ref[cols : 2 * cols, :] = f_ref[...].T.astype(jnp.bfloat16)[0:cols]

    def copies(at):
        slot = lax.rem(at, 2)
        return [
            pltpu.make_async_copy(
                g_ref.at[slot, pl.ds(h * cols, cols), :],
                o_ref.at[:, pl.ds(pl.multiple_of(h * half + at * block, block), block)],
                sem.at[slot, h],
            )
            for h in range(2)
        ]

    @pl.when(step >= 2)
    def _():
        for copy in copies(step - 2):
            copy.wait()

    g = jnp.dot(rt_ref[...], x_ref[...], preferred_element_type=jnp.float32)
    g_ref[lax.rem(step, 2)] = g.astype(g_ref.dtype)
    for copy in copies(step):
        copy.start()

    @pl.when(step == steps - 1)
    def _():
        for copy in copies(step - 1) + copies(step):
            copy.wait()


def backward(returned, x, cols, block=1024):
    rows, half = x.shape
    return pl.pallas_call(
        backward_kernel,
        grid=(half // block,),
        in_specs=[
            pl.BlockSpec((rows // 2, LANES), lambda j: (0, 0)),
            pl.BlockSpec((rows, block), lambda j: (0, j)),
        ],
        out_specs=pl.BlockSpec(memory_space=pl.ANY),
        out_shape=jax.ShapeDtypeStruct((cols, 2 * half), jnp.bfloat16),
        scratch_shapes=[
            pltpu.VMEM((rows, LANES), jnp.float32),
            pltpu.VMEM((rows, LANES), jnp.float32),
            pltpu.VMEM((2 * cols, rows), jnp.bfloat16),
            pltpu.VMEM((2, 2 * cols, block), jnp.bfloat16),
            pltpu.SemaphoreType.DMA((2, 2)),
        ],
    )(returned, x)


def local(expert_hidden, probe_tangent, routed_experts, gate_weights):
    tensor = ("z", "x", "c")
    experts = lax.axis_size("expert")
    parts = lax.axis_size(tensor)
    hidden = expert_hidden[0]
    probe = probe_tangent[0]
    cols = probe.shape[0]
    toks = routed_experts.shape[0]
    capacity = hidden.shape[0] * parts // experts

    x_own = hidden.reshape(2 * hidden.shape[0], hidden.shape[1] // 2)
    x = lax.all_gather(x_own, tensor, axis=0, tiled=True)

    ids = routed_experts.reshape(-1)
    one_hot = (ids[:, None] == jnp.arange(experts, dtype=jnp.int32)[None, :]).astype(jnp.int32)
    earlier = jnp.cumsum(one_hot, axis=0) - one_hot
    rank = jnp.sum(one_hot * earlier, axis=1)
    row = (ids * capacity + rank).reshape(toks, 2)

    tangent = forward(x, probe)
    tangent = lax.all_to_all(
        tangent.reshape(experts, capacity, LANES), "expert", split_axis=0, concat_axis=0, tiled=True
    )
    back, squares = combine(tangent.reshape(experts * capacity, LANES), row, gate_weights)
    back = lax.all_to_all(
        back.reshape(experts, capacity, LANES),
        "expert",
        split_axis=0,
        concat_axis=0,
        tiled=True,
    )
    shares = jnp.broadcast_to(squares[0:1][None], (parts, 1, toks))
    shares = lax.all_to_all(shares, tensor, split_axis=0, concat_axis=0, tiled=True)
    gradient = backward(back.reshape(experts * capacity, LANES), x, cols)
    quadratic = jnp.sum(shares, axis=(0, 1)) / (cols * parts)
    return gradient[None], quadratic


def solution(mesh):
    grid = Mesh(mesh.devices.reshape(8, 8, 4, 2), ("expert", "z", "x", "c"))
    tensor = ("z", "x", "c")
    return jax.shard_map(
        local,
        mesh=grid,
        in_specs=(
            P("expert", tensor, None),
            P("expert", tensor, None),
            P("expert", None),
            P("expert", None),
        ),
        out_specs=(P("expert", tensor, None), P("expert")),
        check_vma=False,
    )
```

```python
import functools

import jax
import jax.numpy as jnp
from jax import lax
from jax.experimental import pallas as pl
from jax.experimental.pallas import tpu as pltpu
from jax.sharding import Mesh, PartitionSpec as P


LANES = 128
WIDTH_A, BLOCKS_A, BLOCKS_B = 1792, 2, 2


def stack_probe(pc_ref, p_ref, start):
    cols, half, width = p_ref.shape[0], p_ref.shape[1] // 2, pc_ref.shape[1]
    pc_ref[...] = jnp.zeros_like(pc_ref)
    pc_ref[0:cols, :] = p_ref[:, start : start + width]
    pc_ref[LANES : LANES + cols, :] = p_ref[:, half + start : half + start + width]


def times(x, y):
    return lax.dot_general(x, y, (((1,), (1,)), ((), ())), preferred_element_type=jnp.float32)


def places(at_ref):
    xs, x, core = 4, at_ref[0], at_ref[1]
    step = 1 - 2 * core
    behind = lax.rem(x - step + xs, xs)
    ahead = lax.rem(x + step + xs, xs)
    across = lax.rem(x + 2, xs)
    return [(x, 0), (behind, 0), (ahead, 0), (across, 4 * core), (across, 4 - 4 * core)]


def forward_b_kernel(start, at_ref, own, near, far, half0, half1, p_ref, y_ref, pc_ref):
    stack_probe(pc_ref, p_ref, start)
    for piece, (x, z) in zip((own, near, far, half0, half1), places(at_ref)):
        zs = piece.shape[0] // 48
        part = times(piece[...], pc_ref[...])
        y_ref[pl.ds(z, zs), :, pl.ds(x, 1)] = part.reshape(zs, 2, 1, 24, 2 * LANES)


def forward_b(at, pieces, probe, start):
    width = pieces[0].shape[1]
    rows = sum(p.shape[0] for p in pieces)
    vmem = pl.BlockSpec(memory_space=pltpu.VMEM)
    return pl.pallas_call(
        functools.partial(forward_b_kernel, start),
        in_specs=[pl.BlockSpec(memory_space=pltpu.SMEM)] + [vmem] * 6,
        out_specs=vmem,
        out_shape=jax.ShapeDtypeStruct((8, 2, 4, 24, 2 * LANES), jnp.float32),
        scratch_shapes=[pltpu.VMEM((2 * LANES, width), jnp.bfloat16)],
        cost_estimate=pl.CostEstimate(
            flops=2 * rows * width * 2 * LANES,
            bytes_accessed=2 * rows * width + 4 * rows * 2 * LANES,
            transcendentals=0,
        ),
    )(at, *pieces, probe)


def forward_a_kernel(x_ref, p_ref, yb_ref, o_ref, pc_ref, y0_ref, y1_ref):
    rows = o_ref.shape[0]

    @pl.when(pl.program_id(0) == 0)
    def _():
        stack_probe(pc_ref, p_ref, 0)

    y = times(x_ref[...], pc_ref[...]) + yb_ref[...]
    y0_ref[...] = y[:, 0:LANES]
    y1_ref[...] = y[:, LANES : 2 * LANES]
    total = y0_ref[pl.ds(0, rows, stride=2), :] + y1_ref[pl.ds(1, rows, stride=2), :]
    o_ref[...] = total.astype(o_ref.dtype)


def forward_a(x, probe, partial, block=384):
    rows, width = x.shape
    return pl.pallas_call(
        forward_a_kernel,
        grid=(rows // block,),
        in_specs=[
            pl.BlockSpec((block, width), lambda i: (i, 0)),
            pl.BlockSpec(probe.shape, lambda i: (0, 0)),
            pl.BlockSpec((block, 2 * LANES), lambda i: (i, 0)),
        ],
        out_specs=pl.BlockSpec((block // 2, LANES), lambda i: (i, 0)),
        out_shape=jax.ShapeDtypeStruct((rows // 2, LANES), jnp.bfloat16),
        scratch_shapes=[
            pltpu.VMEM((2 * LANES, width), jnp.bfloat16),
            pltpu.VMEM((block, LANES), jnp.float32),
            pltpu.VMEM((block, LANES), jnp.float32),
        ],
    )(x, probe, partial)


def combine_kernel(t_ref, row_ref, gate_ref, b_ref, q_ref):
    rows = t_ref.shape[0]
    toks = row_ref.shape[0]
    lane = lax.broadcasted_iota(jnp.int32, (toks, rows), 1)
    zero = jnp.zeros((toks, rows), jnp.bfloat16)
    one = jnp.ones((toks, rows), jnp.bfloat16)
    total = None
    picks = []
    for k in range(2):
        pick = jnp.where(lane == row_ref[:, k : k + 1], one, zero)
        part = jnp.dot(pick, t_ref[...], preferred_element_type=jnp.float32)
        part = part * gate_ref[:, k : k + 1]
        total = part if total is None else total + part
        picks.append(pick)
    back = None
    for k in range(2):
        weighted = (total * gate_ref[:, k : k + 1]).astype(jnp.bfloat16)
        placed = lax.dot_general(
            picks[k], weighted, (((0,), (0,)), ((), ())), preferred_element_type=jnp.float32
        )
        back = placed if back is None else back + placed
    b_ref[...] = back.astype(b_ref.dtype)
    squares = jnp.sum(total * total, axis=1, keepdims=True)
    q_ref[...] = jnp.broadcast_to(squares, (toks, LANES)).T[0:8]


def combine(tangent, row, gate):
    rows = tangent.shape[0]
    toks = row.shape[0]
    return pl.pallas_call(
        combine_kernel,
        out_shape=(
            jax.ShapeDtypeStruct((rows, LANES), jnp.bfloat16),
            jax.ShapeDtypeStruct((8, toks), jnp.float32),
        ),
    )(tangent, row, gate)


def backward_kernel(
    blocks, at_ref, r_ref, a_ref, own, near, far, half0, half1,
    o_ref, e_ref, f_ref, rt_ref, *rest,
):
    rb_refs, (ga_ref, gb_ref, sem) = rest[:5], rest[5:]
    (n_a, w_a), (n_b, w_b) = blocks
    cols, half = o_ref.shape[0], o_ref.shape[1] // 2
    rows = r_ref.shape[0]
    step = pl.program_id(0)

    def turned(ref, first, second):
        ref[0:cols, :] = first.T.astype(jnp.bfloat16)[0:cols]
        ref[cols : 2 * cols, :] = second.T.astype(jnp.bfloat16)[0:cols]

    @pl.when(step == 0)
    def _():
        rf = r_ref[...].astype(jnp.float32)
        zero = jnp.zeros_like(rf)
        e_ref[pl.ds(0, rows, stride=2), :] = rf
        e_ref[pl.ds(1, rows, stride=2), :] = zero
        f_ref[pl.ds(0, rows, stride=2), :] = zero
        f_ref[pl.ds(1, rows, stride=2), :] = rf
        turned(rt_ref, e_ref[...], f_ref[...])

    @pl.when(step == n_a)
    def _():
        for ref, (x, z) in zip(rb_refs, places(at_ref)):
            n = ref.shape[1]
            parts = []
            for src in (e_ref, f_ref):
                view = src.reshape(8, 2, 4, 24, LANES)
                parts.append(view[pl.ds(z, n // 48), :, pl.ds(x, 1)].reshape(n, LANES))
            turned(ref, *parts)

    def copies(at, first, g_ref, width):
        slot = lax.rem(at, 2)
        return [
            pltpu.make_async_copy(
                g_ref.at[slot, pl.ds(h * cols, cols), :],
                o_ref.at[:, pl.ds(pl.multiple_of(h * half + first + at * width, LANES), width)],
                sem.at[slot, h],
            )
            for h in range(2)
        ]

    def phase(here, count, first, g_ref, width, product):
        @pl.when((here >= 2) & (here < count))
        def _():
            for copy in copies(here - 2, first, g_ref, width):
                copy.wait()

        @pl.when((here >= 0) & (here < count))
        def _():
            g_ref[lax.rem(here, 2)] = product().astype(g_ref.dtype)
            for copy in copies(here, first, g_ref, width):
                copy.start()

        @pl.when(here == count - 1)
        def _():
            for back in range(min(2, count)):
                for copy in copies(here - back, first, g_ref, width):
                    copy.wait()

    def product_a():
        return jnp.dot(rt_ref[...], a_ref[...], preferred_element_type=jnp.float32)

    def product_b():
        total = None
        for ref, piece in zip(rb_refs, (own, near, far, half0, half1)):
            part = jnp.dot(ref[...], piece[...], preferred_element_type=jnp.float32)
            total = part if total is None else total + part
        return total

    phase(step, n_a, 0, ga_ref, w_a, product_a)
    phase(step - n_a, n_b, n_a * w_a, gb_ref, w_b, product_b)


def backward(at, returned, a, pieces, cols, n_a, n_b):
    rows, width_a = a.shape
    width_b = pieces[0].shape[1]
    w_a, w_b = width_a // n_a, width_b // n_b
    return pl.pallas_call(
        functools.partial(backward_kernel, ((n_a, w_a), (n_b, w_b))),
        grid=(n_a + n_b,),
        in_specs=[
            pl.BlockSpec(memory_space=pltpu.SMEM),
            pl.BlockSpec((rows // 2, LANES), lambda j: (0, 0)),
            pl.BlockSpec((rows, w_a), lambda j: (0, jnp.minimum(j, n_a - 1))),
        ]
        + [
            pl.BlockSpec((p.shape[0], w_b), lambda j: (0, jnp.maximum(j - n_a, 0))) for p in pieces
        ],
        out_specs=pl.BlockSpec(memory_space=pl.ANY),
        out_shape=jax.ShapeDtypeStruct((cols, 2 * (width_a + width_b)), jnp.bfloat16),
        scratch_shapes=[
            pltpu.VMEM((rows, LANES), jnp.float32),
            pltpu.VMEM((rows, LANES), jnp.float32),
            pltpu.VMEM((2 * cols, rows), jnp.bfloat16),
        ]
        + [pltpu.VMEM((2 * cols, p.shape[0]), jnp.bfloat16) for p in pieces]
        + [
            pltpu.VMEM((2, 2 * cols, w_a), jnp.bfloat16),
            pltpu.VMEM((2, 2 * cols, w_b), jnp.bfloat16),
            pltpu.SemaphoreType.DMA((2, 2)),
        ],
        cost_estimate=pl.CostEstimate(
            flops=2 * rows * (width_a + width_b) * 2 * cols,
            bytes_accessed=2 * rows * (width_a + width_b) + 4 * cols * (width_a + width_b),
            transcendentals=0,
        ),
    )(at, returned, a, *pieces)


def gathered(own, width_a):
    xs = lax.axis_size("x")
    core = lax.axis_index("c")
    own_a, own_b = own[:, :width_a], own[:, width_a:]
    b = lax.all_gather(own_b, ("z", "c"), axis=0, tiled=True)
    a = lax.all_gather(own_a, "x", axis=0, tiled=True)
    a = lax.all_gather(a, ("z", "c"), axis=0, tiled=True)

    onward = [
        (x * 2 + c, (x + 1 - 2 * c) % xs * 2 + c) for x in range(xs) for c in range(2)
    ]
    swap = [(0, 1), (1, 0)]
    near = lax.ppermute(b, ("x", "c"), onward)
    count = near.shape[0] // 2
    half = lax.dynamic_slice_in_dim(near, core * count, count, axis=0)
    half0 = lax.ppermute(half, ("x", "c"), onward)
    far = lax.ppermute(near, "c", swap)
    half1 = lax.ppermute(half0, "c", swap)
    return a, (b, near, far, half0, half1)


def local(expert_hidden, probe_tangent, routed_experts, gate_weights):
    tensor = ("z", "x", "c")
    experts = lax.axis_size("expert")
    parts = lax.axis_size(tensor)
    hidden = expert_hidden[0]
    probe = probe_tangent[0]
    cols = probe.shape[0]
    toks = routed_experts.shape[0]
    capacity = hidden.shape[0] * parts // experts

    own = hidden.reshape(2 * hidden.shape[0], hidden.shape[1] // 2)
    width_a = WIDTH_A
    a, pieces = gathered(own, width_a)
    at = jnp.stack([lax.axis_index("x"), lax.axis_index("c")]).astype(jnp.int32)

    ids = routed_experts.reshape(-1)
    one_hot = (ids[:, None] == jnp.arange(experts, dtype=jnp.int32)[None, :]).astype(jnp.int32)
    earlier = jnp.cumsum(one_hot, axis=0) - one_hot
    rank = jnp.sum(one_hot * earlier, axis=1)
    chip, core, place = rank // 24, rank % 24 // 12, rank % 12
    row = (ids * capacity + core * (capacity // 2) + chip * 12 + place).reshape(toks, 2)

    partial = forward_b(at, pieces, probe, width_a)
    tangent = forward_a(a, probe, partial.reshape(a.shape[0], 2 * LANES))
    tangent = lax.all_to_all(
        tangent.reshape(experts, capacity, LANES), "expert", split_axis=0, concat_axis=0, tiled=True
    )
    back, squares = combine(tangent.reshape(experts * capacity, LANES), row, gate_weights)
    back = lax.all_to_all(
        back.reshape(experts, capacity, LANES),
        "expert",
        split_axis=0,
        concat_axis=0,
        tiled=True,
    )
    shares = lax.all_gather(squares[0:1], ("x", "c"), axis=0, tiled=True)
    shares = jnp.sum(shares, axis=0)
    shares = jnp.broadcast_to(shares[None, None], (lax.axis_size("z"), 1, toks))
    shares = lax.all_to_all(shares, "z", split_axis=0, concat_axis=0, tiled=True)
    gradient = backward(
        at, back.reshape(experts * capacity, LANES), a, pieces, cols, BLOCKS_A, BLOCKS_B
    )
    quadratic = jnp.sum(shares, axis=(0, 1)) / (cols * parts)
    return gradient[None], quadratic


def solution(mesh):
    grid = Mesh(mesh.devices.reshape(8, 8, 4, 2), ("expert", "z", "x", "c"))
    tensor = ("z", "x", "c")
    return jax.shard_map(
        local,
        mesh=grid,
        in_specs=(
            P("expert", tensor, None),
            P("expert", tensor, None),
            P("expert", None),
            P("expert", None),
        ),
        out_specs=(P("expert", tensor, None), P("expert")),
        check_vma=False,
    )
```

```python
import functools

import jax
import jax.numpy as jnp
from jax import lax
from jax.experimental import pallas as pl
from jax.experimental.pallas import tpu as pltpu
from jax.sharding import Mesh, PartitionSpec as P


LANES = 128
WIDTH_A, BLOCKS_A, BLOCKS_B = 2304, 2, 2


def stack_probe(pc_ref, p_ref, start):
    cols, half, width = p_ref.shape[0], p_ref.shape[1] // 2, pc_ref.shape[1]
    pc_ref[...] = jnp.zeros_like(pc_ref)
    pc_ref[0:cols, :] = p_ref[:, start : start + width]
    pc_ref[LANES : LANES + cols, :] = p_ref[:, half + start : half + start + width]


def times(x, y):
    return lax.dot_general(x, y, (((1,), (1,)), ((), ())), preferred_element_type=jnp.float32)


def piece_copies(pieces, all_ref, sem):
    x, core = lax.axis_index("x"), lax.axis_index("c")
    toward = 1 - 2 * core
    behind = lax.rem(x - toward + 4, 4)
    ahead = lax.rem(x + toward + 4, 4)
    across = lax.rem(x + 2, 4)
    other = 1 - core
    spots = (
        (core, x), (other, x), (core, behind), (other, behind),
        (other, ahead), (core, ahead), (core, across), (other, across),
    )
    return [
        pltpu.make_async_copy(piece, all_ref.at[:, c, at], sem.at[i])
        for i, (piece, (c, at)) in enumerate(zip(pieces, spots))
    ]


def forward_b_kernel(start, *refs):
    pieces, (p_ref, y_ref, pc_ref, all_ref, sem) = refs[:8], refs[8:]
    copies = piece_copies(pieces, all_ref, sem)
    for copy in copies:
        copy.start()
    stack_probe(pc_ref, p_ref, start)
    for copy in copies:
        copy.wait()
    width = pc_ref.shape[1]
    rows = 384
    for i in range(y_ref.shape[0] // rows):
        block = all_ref[2 * i : 2 * i + 2].reshape(rows, width)
        y_ref[i * rows : (i + 1) * rows] = times(block, pc_ref[...])


def forward_b(pieces, probe, start):
    width = pieces[0].shape[-1]
    rows = 1536
    return pl.pallas_call(
        functools.partial(forward_b_kernel, start),
        in_specs=[pl.BlockSpec(memory_space=pl.ANY)] * 8
        + [pl.BlockSpec(memory_space=pltpu.VMEM)],
        out_specs=pl.BlockSpec(memory_space=pltpu.VMEM),
        out_shape=jax.ShapeDtypeStruct((rows, 2 * LANES), jnp.float32),
        scratch_shapes=[
            pltpu.VMEM((2 * LANES, width), jnp.bfloat16),
            pltpu.VMEM((8, 2, 4, 24, width), jnp.bfloat16),
            pltpu.SemaphoreType.DMA((8,)),
        ],
        cost_estimate=pl.CostEstimate(
            flops=2 * rows * width * 2 * LANES,
            bytes_accessed=2 * rows * width + 4 * rows * 2 * LANES,
            transcendentals=0,
        ),
    )(*pieces, probe)


def forward_a_kernel(x_ref, p_ref, yb_ref, o_ref, pc_ref, y0_ref, y1_ref):
    rows = o_ref.shape[0]

    @pl.when(pl.program_id(0) == 0)
    def _():
        stack_probe(pc_ref, p_ref, 0)

    y = times(x_ref[...], pc_ref[...]) + yb_ref[...]
    y0_ref[...] = y[:, 0:LANES]
    y1_ref[...] = y[:, LANES : 2 * LANES]
    total = y0_ref[pl.ds(0, rows, stride=2), :] + y1_ref[pl.ds(1, rows, stride=2), :]
    o_ref[...] = total.astype(o_ref.dtype)


def forward_a(x, probe, partial, block=384):
    rows, width = x.shape
    return pl.pallas_call(
        forward_a_kernel,
        grid=(rows // block,),
        in_specs=[
            pl.BlockSpec((block, width), lambda i: (i, 0)),
            pl.BlockSpec(probe.shape, lambda i: (0, 0)),
            pl.BlockSpec((block, 2 * LANES), lambda i: (i, 0)),
        ],
        out_specs=pl.BlockSpec((block // 2, LANES), lambda i: (i, 0)),
        out_shape=jax.ShapeDtypeStruct((rows // 2, LANES), jnp.bfloat16),
        scratch_shapes=[
            pltpu.VMEM((2 * LANES, width), jnp.bfloat16),
            pltpu.VMEM((block, LANES), jnp.float32),
            pltpu.VMEM((block, LANES), jnp.float32),
        ],
    )(x, probe, partial)


def combine_kernel(capacity, t_ref, id_ref, gate_ref, b_ref, q_ref):
    rows = t_ref.shape[0]
    toks = id_ref.shape[1]
    experts = lax.broadcasted_iota(jnp.int32, (8, toks), 0)
    named = [(experts == id_ref[k : k + 1, :]).astype(jnp.float32) for k in range(2)]
    before = lax.broadcasted_iota(jnp.int32, (toks, toks), 0)
    before = before < lax.broadcasted_iota(jnp.int32, (toks, toks), 1)
    counts = jnp.dot(
        (named[0] + named[1]).astype(jnp.bfloat16),
        before.astype(jnp.float32).astype(jnp.bfloat16),
        preferred_element_type=jnp.float32,
    )
    place = lax.broadcasted_iota(jnp.int32, (rows, toks), 0)
    picks = []
    total = None
    for k in range(2):
        rank = jnp.sum(named[k] * counts, axis=0, keepdims=True).astype(jnp.int32)
        dozen = jnp.right_shift(rank * 5462, 16)
        slot = (dozen & 1) * (capacity // 2) + jnp.right_shift(dozen, 1) * 12 + rank - dozen * 12
        row = id_ref[k : k + 1, :] * capacity + slot
        pick = (place == row).astype(jnp.float32).astype(jnp.bfloat16)
        part = lax.dot_general(
            t_ref[...], pick, (((0,), (0,)), ((), ())), preferred_element_type=jnp.float32
        )
        part = part * gate_ref[k : k + 1, :]
        total = part if total is None else total + part
        picks.append(pick)
    back = None
    for k in range(2):
        weighted = (total * gate_ref[k : k + 1, :]).astype(jnp.bfloat16)
        placed = lax.dot_general(
            picks[k], weighted, (((1,), (1,)), ((), ())), preferred_element_type=jnp.float32
        )
        back = placed if back is None else back + placed
    b_ref[...] = back.astype(b_ref.dtype)
    q_ref[...] = jnp.sum(total * total, axis=0, keepdims=True)


def combine(tangent, ids, gates, capacity):
    rows = tangent.shape[0]
    toks = ids.shape[1]
    return pl.pallas_call(
        functools.partial(combine_kernel, capacity),
        out_shape=(
            jax.ShapeDtypeStruct((rows, LANES), jnp.bfloat16),
            jax.ShapeDtypeStruct((1, toks), jnp.float32),
        ),
    )(tangent, ids, gates)


def backward_kernel(blocks, r_ref, a_ref, *refs):
    pieces, (o_ref, e_ref, f_ref, rt_ref, all_ref, ga_ref, gb_ref, in_sem, sem) = refs[:8], refs[8:]
    (n_a, w_a), (n_b, w_b) = blocks
    cols, half = o_ref.shape[0], o_ref.shape[1] // 2
    rows = r_ref.shape[0]
    step = pl.program_id(0)
    arrivals = piece_copies(pieces, all_ref, in_sem)

    @pl.when(step == 0)
    def _():
        for copy in arrivals:
            copy.start()
        rf = r_ref[...].astype(jnp.float32)
        zero = jnp.zeros_like(rf)
        e_ref[pl.ds(0, rows, stride=2), :] = rf
        e_ref[pl.ds(1, rows, stride=2), :] = zero
        f_ref[pl.ds(0, rows, stride=2), :] = zero
        f_ref[pl.ds(1, rows, stride=2), :] = rf
        rt_ref[0:cols, :] = e_ref[...].T.astype(jnp.bfloat16)[0:cols]
        rt_ref[cols : 2 * cols, :] = f_ref[...].T.astype(jnp.bfloat16)[0:cols]

    @pl.when(step == n_a)
    def _():
        for copy in arrivals:
            copy.wait()

    def copies(at, first, g_ref, width):
        slot = at % 2 if isinstance(at, int) else lax.rem(at, 2)
        return [
            pltpu.make_async_copy(
                g_ref.at[slot, pl.ds(h * cols, cols), :],
                o_ref.at[:, pl.ds(pl.multiple_of(h * half + first + at * width, LANES), width)],
                sem.at[slot, h],
            )
            for h in range(2)
        ]

    def phase(here, count, first, g_ref, width, product):
        @pl.when((here >= 2) & (here < count))
        def _():
            for copy in copies(here - 2, first, g_ref, width):
                copy.wait()

        @pl.when((here >= 0) & (here < count))
        def _():
            g_ref[lax.rem(here, 2)] = product().astype(g_ref.dtype)
            for copy in copies(here, first, g_ref, width):
                copy.start()

        @pl.when(here == count - 1)
        def _():
            for back in range(min(2, count)):
                for copy in copies(here - back, first, g_ref, width):
                    copy.wait()

    def product_a():
        return jnp.dot(rt_ref[...], a_ref[...], preferred_element_type=jnp.float32)

    def product_b():
        at = pl.multiple_of((step - n_a) * w_b, LANES)
        block = all_ref[:, :, :, :, pl.ds(at, w_b)].reshape(2 * rows, w_b)
        return jnp.dot(rt_ref[...], block, preferred_element_type=jnp.float32)

    phase(step, n_a, 0, ga_ref, w_a, product_a)
    phase(step - n_a, n_b, n_a * w_a, gb_ref, w_b, product_b)


def backward(returned, a, pieces, cols, n_a, n_b):
    rows, width_a = a.shape
    width_b = pieces[0].shape[-1]
    w_a, w_b = width_a // n_a, width_b // n_b
    return pl.pallas_call(
        functools.partial(backward_kernel, ((n_a, w_a), (n_b, w_b))),
        grid=(n_a + n_b,),
        in_specs=[
            pl.BlockSpec((rows // 2, LANES), lambda j: (0, 0)),
            pl.BlockSpec((rows, w_a), lambda j: (0, jnp.minimum(j, n_a - 1))),
        ]
        + [pl.BlockSpec(memory_space=pl.ANY)] * 8,
        out_specs=pl.BlockSpec(memory_space=pl.ANY),
        out_shape=jax.ShapeDtypeStruct((cols, 2 * (width_a + width_b)), jnp.bfloat16),
        scratch_shapes=[
            pltpu.VMEM((rows, LANES), jnp.float32),
            pltpu.VMEM((rows, LANES), jnp.float32),
            pltpu.VMEM((2 * cols, rows), jnp.bfloat16),
            pltpu.VMEM((8, 2, 4, 24, width_b), jnp.bfloat16),
            pltpu.VMEM((2, 2 * cols, w_a), jnp.bfloat16),
            pltpu.VMEM((2, 2 * cols, w_b), jnp.bfloat16),
            pltpu.SemaphoreType.DMA((8,)),
            pltpu.SemaphoreType.DMA((2, 2)),
        ],
        cost_estimate=pl.CostEstimate(
            flops=2 * rows * (width_a + width_b) * 2 * cols,
            bytes_accessed=2 * rows * (width_a + width_b) + 4 * cols * (width_a + width_b),
            transcendentals=0,
        ),
    )(returned, a, *pieces)


def gathered(own, width_a):
    xs, zs = lax.axis_size("x"), lax.axis_size("z")
    a = lax.all_gather(own[:, :width_a], "x", axis=0, tiled=True)
    copies = jnp.broadcast_to(own[None, :, width_a:], (zs, own.shape[0], own.shape[1] - width_a))
    copies, a = lax.optimization_barrier((copies, a))
    a = lax.all_gather(a, ("z", "c"), axis=0, tiled=True)
    b = lax.all_to_all(copies, "z", split_axis=0, concat_axis=0, tiled=True)

    onward = [(x * 2 + c, (x + 1 - 2 * c) % xs * 2 + c) for x in range(xs) for c in range(2)]

    def send(v):
        return lax.ppermute(v, ("x", "c"), onward)

    def swap(v):
        return lax.ppermute(v, "c", [(0, 1), (1, 0)])

    near0 = send(b)
    mate = swap(b)
    near1 = send(mate)
    across = send(near0)
    far0, far1 = swap(near0), swap(near1)
    return a, (b, mate, near0, near1, far0, far1, across, swap(across))


def local(expert_hidden, probe_tangent, routed_experts, gate_weights):
    tensor = ("z", "x", "c")
    experts = lax.axis_size("expert")
    parts = lax.axis_size(tensor)
    hidden = expert_hidden[0]
    probe = probe_tangent[0]
    cols = probe.shape[0]
    toks = routed_experts.shape[0]
    capacity = hidden.shape[0] * parts // experts

    own = hidden.reshape(2 * hidden.shape[0], hidden.shape[1] // 2)
    width_a = WIDTH_A
    a, pieces = gathered(own, width_a)
    partial = forward_b(pieces, probe, width_a)
    tangent = forward_a(a, probe, partial)
    tangent = lax.all_to_all(
        tangent.reshape(experts, capacity, LANES), "expert", split_axis=0, concat_axis=0, tiled=True
    )
    back, squares = combine(
        tangent.reshape(experts * capacity, LANES), routed_experts.T, gate_weights.T, capacity
    )
    back = lax.all_to_all(
        back.reshape(experts, capacity, LANES),
        "expert",
        split_axis=0,
        concat_axis=0,
        tiled=True,
    )
    shares = lax.all_gather(squares, ("x", "c"), axis=0, tiled=True)
    shares = jnp.sum(shares, axis=0)
    shares = jnp.broadcast_to(shares[None, None], (lax.axis_size("z"), 1, toks))
    shares = lax.all_to_all(shares, "z", split_axis=0, concat_axis=0, tiled=True)
    gradient = backward(
        back.reshape(experts * capacity, LANES), a, pieces, cols, BLOCKS_A, BLOCKS_B
    )
    quadratic = jnp.sum(shares, axis=(0, 1)) / (cols * parts)
    return gradient[None], quadratic


def solution(mesh):
    grid = Mesh(mesh.devices.reshape(8, 8, 4, 2), ("expert", "z", "x", "c"))
    tensor = ("z", "x", "c")
    return jax.shard_map(
        local,
        mesh=grid,
        in_specs=(
            P("expert", tensor, None),
            P("expert", tensor, None),
            P("expert", None),
            P("expert", None),
        ),
        out_specs=(P("expert", tensor, None), P("expert")),
        check_vma=False,
    )
```

```python
import functools

import jax
import jax.numpy as jnp
from jax import lax
from jax.experimental import pallas as pl
from jax.experimental.pallas import tpu as pltpu
from jax.sharding import Mesh, PartitionSpec as P


LANES = 128
WIDTH_A, BLOCKS_A, BLOCKS_B = 2304, 2, 2
PIECES = 10


def stack_probe(pc_ref, p_ref, start):
    cols, half, width = p_ref.shape[0], p_ref.shape[1] // 2, pc_ref.shape[1]
    pc_ref[...] = jnp.zeros_like(pc_ref)
    pc_ref[0:cols, :] = p_ref[:, start : start + width]
    pc_ref[LANES : LANES + cols, :] = p_ref[:, half + start : half + start + width]


def times(x, y):
    return lax.dot_general(x, y, (((1,), (1,)), ((), ())), preferred_element_type=jnp.float32)


def piece_copies(pieces, all_ref, sem):
    x, core = lax.axis_index("x"), lax.axis_index("c")
    other = 1 - core
    before, after, across = (x + 3) & 3, (x + 1) & 3, (x + 2) & 3
    spots = (
        (0, core, x), (0, other, x),
        (0, core, before), (0, core, after), (0, core, across), (4, core, across),
        (0, other, before), (0, other, after), (0, other, across), (4, other, across),
    )
    return [
        pltpu.make_async_copy(piece, all_ref.at[z : z + piece.shape[0], c, at], sem.at[i])
        for i, (piece, (z, c, at)) in enumerate(zip(pieces, spots))
    ]


def forward_b_kernel(start, *refs):
    pieces, (p_ref, y_ref, pc_ref, all_ref, sem) = refs[:PIECES], refs[PIECES:]
    copies = piece_copies(pieces, all_ref, sem)
    for copy in copies:
        copy.start()
    stack_probe(pc_ref, p_ref, start)
    for copy in copies:
        copy.wait()
    width = pc_ref.shape[1]
    rows = 384
    for i in range(y_ref.shape[0] // rows):
        block = all_ref[2 * i : 2 * i + 2].reshape(rows, width)
        y_ref[i * rows : (i + 1) * rows] = times(block, pc_ref[...])


def forward_b(pieces, probe, start):
    width = pieces[0].shape[-1]
    rows = 1536
    return pl.pallas_call(
        functools.partial(forward_b_kernel, start),
        in_specs=[pl.BlockSpec(memory_space=pl.ANY)] * PIECES
        + [pl.BlockSpec(memory_space=pltpu.VMEM)],
        out_specs=pl.BlockSpec(memory_space=pltpu.VMEM),
        out_shape=jax.ShapeDtypeStruct((rows, 2 * LANES), jnp.float32),
        scratch_shapes=[
            pltpu.VMEM((2 * LANES, width), jnp.bfloat16),
            pltpu.VMEM((8, 2, 4, 24, width), jnp.bfloat16),
            pltpu.SemaphoreType.DMA((PIECES,)),
        ],
        cost_estimate=pl.CostEstimate(
            flops=2 * rows * width * 2 * LANES,
            bytes_accessed=2 * rows * width + 4 * rows * 2 * LANES,
            transcendentals=0,
        ),
    )(*pieces, probe)


def forward_a_kernel(x_ref, p_ref, yb_ref, o_ref, pc_ref, y0_ref, y1_ref):
    rows = o_ref.shape[0]

    @pl.when(pl.program_id(0) == 0)
    def _():
        stack_probe(pc_ref, p_ref, 0)

    y = times(x_ref[...], pc_ref[...]) + yb_ref[...]
    y0_ref[...] = y[:, 0:LANES]
    y1_ref[...] = y[:, LANES : 2 * LANES]
    total = y0_ref[pl.ds(0, rows, stride=2), :] + y1_ref[pl.ds(1, rows, stride=2), :]
    o_ref[...] = total.astype(o_ref.dtype)


def forward_a(x, probe, partial, block=384):
    rows, width = x.shape
    return pl.pallas_call(
        forward_a_kernel,
        grid=(rows // block,),
        in_specs=[
            pl.BlockSpec((block, width), lambda i: (i, 0)),
            pl.BlockSpec(probe.shape, lambda i: (0, 0)),
            pl.BlockSpec((block, 2 * LANES), lambda i: (i, 0)),
        ],
        out_specs=pl.BlockSpec((block // 2, LANES), lambda i: (i, 0)),
        out_shape=jax.ShapeDtypeStruct((rows // 2, LANES), jnp.bfloat16),
        scratch_shapes=[
            pltpu.VMEM((2 * LANES, width), jnp.bfloat16),
            pltpu.VMEM((block, LANES), jnp.float32),
            pltpu.VMEM((block, LANES), jnp.float32),
        ],
    )(x, probe, partial)


def combine_kernel(capacity, t_ref, id_ref, gate_ref, b_ref, q_ref):
    rows = t_ref.shape[0]
    toks = id_ref.shape[1]
    experts = lax.broadcasted_iota(jnp.int32, (8, toks), 0)
    named = [(experts == id_ref[k : k + 1, :]).astype(jnp.float32) for k in range(2)]
    before = lax.broadcasted_iota(jnp.int32, (toks, toks), 0)
    before = before < lax.broadcasted_iota(jnp.int32, (toks, toks), 1)
    counts = jnp.dot(
        (named[0] + named[1]).astype(jnp.bfloat16),
        before.astype(jnp.float32).astype(jnp.bfloat16),
        preferred_element_type=jnp.float32,
    )
    place = lax.broadcasted_iota(jnp.int32, (rows, toks), 0)
    picks = []
    total = None
    for k in range(2):
        rank = jnp.sum(named[k] * counts, axis=0, keepdims=True).astype(jnp.int32)
        dozen = jnp.right_shift(rank * 5462, 16)
        slot = (dozen & 1) * (capacity // 2) + jnp.right_shift(dozen, 1) * 12 + rank - dozen * 12
        row = id_ref[k : k + 1, :] * capacity + slot
        pick = (place == row).astype(jnp.float32).astype(jnp.bfloat16)
        part = lax.dot_general(
            t_ref[...], pick, (((0,), (0,)), ((), ())), preferred_element_type=jnp.float32
        )
        part = part * gate_ref[k : k + 1, :]
        total = part if total is None else total + part
        picks.append(pick)
    back = None
    for k in range(2):
        weighted = (total * gate_ref[k : k + 1, :]).astype(jnp.bfloat16)
        placed = lax.dot_general(
            picks[k], weighted, (((1,), (1,)), ((), ())), preferred_element_type=jnp.float32
        )
        back = placed if back is None else back + placed
    b_ref[...] = back.astype(b_ref.dtype)
    q_ref[...] = jnp.sum(total * total, axis=0, keepdims=True)


def combine(tangent, ids, gates, capacity):
    rows = tangent.shape[0]
    toks = ids.shape[1]
    return pl.pallas_call(
        functools.partial(combine_kernel, capacity),
        out_shape=(
            jax.ShapeDtypeStruct((rows, LANES), jnp.bfloat16),
            jax.ShapeDtypeStruct((1, toks), jnp.float32),
        ),
    )(tangent, ids, gates)


def backward_kernel(blocks, r_ref, a_ref, *refs):
    pieces, (o_ref, e_ref, f_ref, rt_ref, all_ref, ga_ref, gb_ref, in_sem, sem) = refs[:PIECES], refs[PIECES:]
    (n_a, w_a), (n_b, w_b) = blocks
    cols, half = o_ref.shape[0], o_ref.shape[1] // 2
    rows = r_ref.shape[0]
    step = pl.program_id(0)
    arrivals = piece_copies(pieces, all_ref, in_sem)

    @pl.when(step == 0)
    def _():
        for copy in arrivals:
            copy.start()
        rf = r_ref[...].astype(jnp.float32)
        zero = jnp.zeros_like(rf)
        e_ref[pl.ds(0, rows, stride=2), :] = rf
        e_ref[pl.ds(1, rows, stride=2), :] = zero
        f_ref[pl.ds(0, rows, stride=2), :] = zero
        f_ref[pl.ds(1, rows, stride=2), :] = rf
        rt_ref[0:cols, :] = e_ref[...].T.astype(jnp.bfloat16)[0:cols]
        rt_ref[cols : 2 * cols, :] = f_ref[...].T.astype(jnp.bfloat16)[0:cols]

    @pl.when(step == n_a)
    def _():
        for copy in arrivals:
            copy.wait()

    def copies(at, first, g_ref, width):
        slot = at % 2 if isinstance(at, int) else lax.rem(at, 2)
        return [
            pltpu.make_async_copy(
                g_ref.at[slot, pl.ds(h * cols, cols), :],
                o_ref.at[:, pl.ds(pl.multiple_of(h * half + first + at * width, LANES), width)],
                sem.at[slot, h],
            )
            for h in range(2)
        ]

    def phase(here, count, first, g_ref, width, product):
        @pl.when((here >= 2) & (here < count))
        def _():
            for copy in copies(here - 2, first, g_ref, width):
                copy.wait()

        @pl.when((here >= 0) & (here < count))
        def _():
            g_ref[lax.rem(here, 2)] = product().astype(g_ref.dtype)
            for copy in copies(here, first, g_ref, width):
                copy.start()

        @pl.when(here == count - 1)
        def _():
            for back in range(min(2, count)):
                for copy in copies(here - back, first, g_ref, width):
                    copy.wait()

    def product_a():
        return jnp.dot(rt_ref[...], a_ref[...], preferred_element_type=jnp.float32)

    def product_b():
        at = pl.multiple_of((step - n_a) * w_b, LANES)
        block = all_ref[:, :, :, :, pl.ds(at, w_b)].reshape(2 * rows, w_b)
        return jnp.dot(rt_ref[...], block, preferred_element_type=jnp.float32)

    phase(step, n_a, 0, ga_ref, w_a, product_a)
    phase(step - n_a, n_b, n_a * w_a, gb_ref, w_b, product_b)


def backward(returned, a, pieces, cols, n_a, n_b):
    rows, width_a = a.shape
    width_b = pieces[0].shape[-1]
    w_a, w_b = width_a // n_a, width_b // n_b
    return pl.pallas_call(
        functools.partial(backward_kernel, ((n_a, w_a), (n_b, w_b))),
        grid=(n_a + n_b,),
        in_specs=[
            pl.BlockSpec((rows // 2, LANES), lambda j: (0, 0)),
            pl.BlockSpec((rows, w_a), lambda j: (0, jnp.minimum(j, n_a - 1))),
        ]
        + [pl.BlockSpec(memory_space=pl.ANY)] * PIECES,
        out_specs=pl.BlockSpec(memory_space=pl.ANY),
        out_shape=jax.ShapeDtypeStruct((cols, 2 * (width_a + width_b)), jnp.bfloat16),
        scratch_shapes=[
            pltpu.VMEM((rows, LANES), jnp.float32),
            pltpu.VMEM((rows, LANES), jnp.float32),
            pltpu.VMEM((2 * cols, rows), jnp.bfloat16),
            pltpu.VMEM((8, 2, 4, 24, width_b), jnp.bfloat16),
            pltpu.VMEM((2, 2 * cols, w_a), jnp.bfloat16),
            pltpu.VMEM((2, 2 * cols, w_b), jnp.bfloat16),
            pltpu.SemaphoreType.DMA((PIECES,)),
            pltpu.SemaphoreType.DMA((2, 2)),
        ],
        cost_estimate=pl.CostEstimate(
            flops=2 * rows * (width_a + width_b) * 2 * cols,
            bytes_accessed=2 * rows * (width_a + width_b) + 4 * cols * (width_a + width_b),
            transcendentals=0,
        ),
    )(returned, a, *pieces)


def gathered(own, width_a):
    xs = lax.axis_size("x")
    a, own_b = own[:, :width_a], own[:, width_a:]
    b = jnp.broadcast_to(own_b[None], (lax.axis_size("z"),) + own_b.shape)
    b = lax.all_to_all(b, "z", split_axis=0, concat_axis=0, tiled=True)
    a = lax.all_gather(a, "x", axis=0, tiled=True)
    a = lax.all_gather(a, ("z", "c"), axis=0, tiled=True)

    def send(v, step):
        return lax.ppermute(v, "x", [(i, (i + step) % xs) for i in range(xs)])

    def swap(v):
        return lax.ppermute(v, "c", [(0, 1), (1, 0)])

    half = b.shape[0] // 2
    fore, back = send(b, 1), send(b, -1)
    mate = swap(b)
    on0, on1 = send(fore[:half], 1), send(back[half:], -1)
    mates = [swap(v) for v in (fore, back, on0, on1)]
    return a, (b, mate, fore, back, on0, on1, *mates)


def local(expert_hidden, probe_tangent, routed_experts, gate_weights):
    tensor = ("z", "x", "c")
    experts = lax.axis_size("expert")
    parts = lax.axis_size(tensor)
    hidden = expert_hidden[0]
    probe = probe_tangent[0]
    cols = probe.shape[0]
    toks = routed_experts.shape[0]
    capacity = hidden.shape[0] * parts // experts

    own = hidden.reshape(2 * hidden.shape[0], hidden.shape[1] // 2)
    width_a = WIDTH_A
    a, pieces = gathered(own, width_a)
    partial = forward_b(pieces, probe, width_a)
    tangent = forward_a(a, probe, partial)
    tangent = lax.all_to_all(
        tangent.reshape(experts, capacity, LANES), "expert", split_axis=0, concat_axis=0, tiled=True
    )
    back, squares = combine(
        tangent.reshape(experts * capacity, LANES), routed_experts.T, gate_weights.T, capacity
    )
    back = lax.all_to_all(
        back.reshape(experts, capacity, LANES),
        "expert",
        split_axis=0,
        concat_axis=0,
        tiled=True,
    )
    shares = lax.all_gather(squares, "x", axis=0, tiled=True)
    shares = jnp.sum(shares, axis=0)
    shares = jnp.broadcast_to(shares[None, None], (lax.axis_size(("z", "c")), 1, toks))
    shares = lax.all_to_all(shares, ("z", "c"), split_axis=0, concat_axis=0, tiled=True)
    gradient = backward(
        back.reshape(experts * capacity, LANES), a, pieces, cols, BLOCKS_A, BLOCKS_B
    )
    quadratic = jnp.sum(shares, axis=(0, 1)) / (cols * parts)
    return gradient[None], quadratic


def solution(mesh):
    grid = Mesh(mesh.devices.reshape(8, 8, 4, 2), ("expert", "z", "x", "c"))
    tensor = ("z", "x", "c")
    return jax.shard_map(
        local,
        mesh=grid,
        in_specs=(
            P("expert", tensor, None),
            P("expert", tensor, None),
            P("expert", None),
            P("expert", None),
        ),
        out_specs=(P("expert", tensor, None), P("expert")),
        check_vma=False,
    )
```

```python
import functools

import jax
import jax.numpy as jnp
from jax import lax
from jax.experimental import pallas as pl
from jax.experimental.pallas import tpu as pltpu
from jax.sharding import Mesh, PartitionSpec as P


LANES = 128
WIDTH_A, BLOCKS_A, BLOCKS_B = 2304, 2, 1
PIECES = 10


def stack_probe(pc_ref, p_ref, start):
    cols, half, width = p_ref.shape[0], p_ref.shape[1] // 2, pc_ref.shape[1]
    pc_ref[...] = jnp.zeros_like(pc_ref)
    pc_ref[0:cols, :] = p_ref[:, start : start + width]
    pc_ref[LANES : LANES + cols, :] = p_ref[:, half + start : half + start + width]


def stack_copies(pc_ref, p_ref, start, sem):
    cols, half, width = p_ref.shape[0], p_ref.shape[1] // 2, pc_ref.shape[1]
    return [
        pltpu.make_async_copy(
            p_ref.at[:, h * half + start : h * half + start + width],
            pc_ref.at[h * LANES : h * LANES + cols, :],
            sem.at[h],
        )
        for h in range(2)
    ]


def clear_rest(pc_ref, cols):
    for h in range(2):
        rest = pc_ref.at[h * LANES + cols : (h + 1) * LANES]
        rest[...] = jnp.zeros(rest.shape, rest.dtype)


def times(x, y):
    return lax.dot_general(x, y, (((1,), (1,)), ((), ())), preferred_element_type=jnp.float32)


def piece_copies(pieces, all_ref, sem):
    x, core = lax.axis_index("x"), lax.axis_index("c")
    other = 1 - core
    before, after, across = (x + 3) & 3, (x + 1) & 3, (x + 2) & 3
    spots = (
        (0, core, x), (0, other, x),
        (0, core, before), (0, core, after), (0, core, across), (4, core, across),
        (0, other, before), (0, other, after), (0, other, across), (4, other, across),
    )
    return [
        pltpu.make_async_copy(piece, all_ref.at[z : z + piece.shape[0], c, at], sem.at[i])
        for i, (piece, (z, c, at)) in enumerate(zip(pieces, spots))
    ]


def forward_b_kernel(start, *refs):
    pieces, (p_ref, y_ref, pc_ref, all_ref, sem, p_sem) = refs[:PIECES], refs[PIECES:]
    copies = stack_copies(pc_ref, p_ref, start, p_sem) + piece_copies(pieces, all_ref, sem)
    for copy in copies:
        copy.start()
    clear_rest(pc_ref, p_ref.shape[0])
    for copy in copies:
        copy.wait()
    width = pc_ref.shape[1]
    rows = 384
    for i in range(y_ref.shape[0] // rows):
        block = all_ref[2 * i : 2 * i + 2].reshape(rows, width)
        y_ref[i * rows : (i + 1) * rows] = times(block, pc_ref[...])


def forward_b(pieces, probe, start):
    width = pieces[0].shape[-1]
    rows = 1536
    return pl.pallas_call(
        functools.partial(forward_b_kernel, start),
        in_specs=[pl.BlockSpec(memory_space=pltpu.VMEM)] * PIECES
        + [pl.BlockSpec(memory_space=pl.ANY)],
        out_specs=pl.BlockSpec(memory_space=pltpu.VMEM),
        out_shape=jax.ShapeDtypeStruct((rows, 2 * LANES), jnp.float32),
        scratch_shapes=[
            pltpu.VMEM((2 * LANES, width), jnp.bfloat16),
            pltpu.VMEM((8, 2, 4, 24, width), jnp.bfloat16),
            pltpu.SemaphoreType.DMA((PIECES,)),
            pltpu.SemaphoreType.DMA((2,)),
        ],
        cost_estimate=pl.CostEstimate(
            flops=2 * rows * width * 2 * LANES,
            bytes_accessed=2 * rows * width + 4 * rows * 2 * LANES,
            transcendentals=0,
        ),
    )(*pieces, probe)


def forward_a_kernel(x_ref, p_ref, yb_ref, o_ref, pc_ref, y0_ref, y1_ref):
    rows = o_ref.shape[0]

    @pl.when(pl.program_id(0) == 0)
    def _():
        stack_probe(pc_ref, p_ref, 0)

    y = times(x_ref[...], pc_ref[...]) + yb_ref[...]
    y0_ref[...] = y[:, 0:LANES]
    y1_ref[...] = y[:, LANES : 2 * LANES]
    total = y0_ref[pl.ds(0, rows, stride=2), :] + y1_ref[pl.ds(1, rows, stride=2), :]
    o_ref[...] = total.astype(o_ref.dtype)


def forward_a(x, probe, partial, block=384):
    rows, width = x.shape
    return pl.pallas_call(
        forward_a_kernel,
        grid=(rows // block,),
        in_specs=[
            pl.BlockSpec((block, width), lambda i: (i, 0)),
            pl.BlockSpec(probe.shape, lambda i: (0, 0)),
            pl.BlockSpec((block, 2 * LANES), lambda i: (i, 0)),
        ],
        out_specs=pl.BlockSpec((block // 2, LANES), lambda i: (i, 0)),
        out_shape=jax.ShapeDtypeStruct((rows // 2, LANES), jnp.bfloat16),
        scratch_shapes=[
            pltpu.VMEM((2 * LANES, width), jnp.bfloat16),
            pltpu.VMEM((block, LANES), jnp.float32),
            pltpu.VMEM((block, LANES), jnp.float32),
        ],
    )(x, probe, partial)


def combine_kernel(capacity, t_ref, id_ref, gate_ref, b_ref, q_ref):
    rows = t_ref.shape[0]
    toks = id_ref.shape[1]
    experts = lax.broadcasted_iota(jnp.int32, (8, toks), 0)
    named = [(experts == id_ref[k : k + 1, :]).astype(jnp.float32) for k in range(2)]
    before = lax.broadcasted_iota(jnp.int32, (toks, toks), 0)
    before = before < lax.broadcasted_iota(jnp.int32, (toks, toks), 1)
    counts = jnp.dot(
        (named[0] + named[1]).astype(jnp.bfloat16),
        before.astype(jnp.float32).astype(jnp.bfloat16),
        preferred_element_type=jnp.float32,
    )
    place = lax.broadcasted_iota(jnp.int32, (rows, toks), 0)
    picks = []
    total = None
    for k in range(2):
        rank = jnp.sum(named[k] * counts, axis=0, keepdims=True).astype(jnp.int32)
        dozen = jnp.right_shift(rank * 5462, 16)
        slot = (dozen & 1) * (capacity // 2) + jnp.right_shift(dozen, 1) * 12 + rank - dozen * 12
        row = id_ref[k : k + 1, :] * capacity + slot
        pick = (place == row).astype(jnp.float32).astype(jnp.bfloat16)
        part = lax.dot_general(
            t_ref[...], pick, (((0,), (0,)), ((), ())), preferred_element_type=jnp.float32
        )
        part = part * gate_ref[k : k + 1, :]
        total = part if total is None else total + part
        picks.append(pick)
    back = None
    for k in range(2):
        weighted = (total * gate_ref[k : k + 1, :]).astype(jnp.bfloat16)
        placed = lax.dot_general(
            picks[k], weighted, (((1,), (1,)), ((), ())), preferred_element_type=jnp.float32
        )
        back = placed if back is None else back + placed
    b_ref[...] = back.astype(b_ref.dtype)
    q_ref[...] = jnp.sum(total * total, axis=0, keepdims=True)


def combine(tangent, ids, gates, capacity):
    rows = tangent.shape[0]
    toks = ids.shape[1]
    return pl.pallas_call(
        functools.partial(combine_kernel, capacity),
        out_shape=(
            jax.ShapeDtypeStruct((rows, LANES), jnp.bfloat16),
            jax.ShapeDtypeStruct((1, toks), jnp.float32),
        ),
    )(tangent, ids, gates)


def backward_kernel(blocks, r_ref, a_ref, *refs):
    pieces, (o_ref, e_ref, f_ref, rt_ref, all_ref, ga_ref, gb_ref, in_sem, sem) = refs[:PIECES], refs[PIECES:]
    (n_a, w_a), (n_b, w_b) = blocks
    cols, half = o_ref.shape[0], o_ref.shape[1] // 2
    rows = r_ref.shape[0]
    step = pl.program_id(0)
    arrivals = piece_copies(pieces, all_ref, in_sem)

    @pl.when(step == 0)
    def _():
        for copy in arrivals:
            copy.start()
        rf = r_ref[...].astype(jnp.float32)
        zero = jnp.zeros_like(rf)
        e_ref[pl.ds(0, rows, stride=2), :] = rf
        e_ref[pl.ds(1, rows, stride=2), :] = zero
        f_ref[pl.ds(0, rows, stride=2), :] = zero
        f_ref[pl.ds(1, rows, stride=2), :] = rf
        rt_ref[0:cols, :] = e_ref[...].T.astype(jnp.bfloat16)[0:cols]
        rt_ref[cols : 2 * cols, :] = f_ref[...].T.astype(jnp.bfloat16)[0:cols]

    @pl.when(step == n_a)
    def _():
        for copy in arrivals:
            copy.wait()

    def copies(at, first, g_ref, width):
        slot = at % 2 if isinstance(at, int) else lax.rem(at, 2)
        return [
            pltpu.make_async_copy(
                g_ref.at[slot, pl.ds(h * cols, cols), :],
                o_ref.at[:, pl.ds(pl.multiple_of(h * half + first + at * width, LANES), width)],
                sem.at[slot, h],
            )
            for h in range(2)
        ]

    def phase(here, count, first, g_ref, width, product):
        @pl.when((here >= 2) & (here < count))
        def _():
            for copy in copies(here - 2, first, g_ref, width):
                copy.wait()

        @pl.when((here >= 0) & (here < count))
        def _():
            g_ref[lax.rem(here, 2)] = product().astype(g_ref.dtype)
            for copy in copies(here, first, g_ref, width):
                copy.start()

        @pl.when(here == count - 1)
        def _():
            for back in range(min(2, count)):
                for copy in copies(here - back, first, g_ref, width):
                    copy.wait()

    def product_a():
        return jnp.dot(rt_ref[...], a_ref[...], preferred_element_type=jnp.float32)

    def product_b():
        at = pl.multiple_of((step - n_a) * w_b, LANES)
        block = all_ref[:, :, :, :, pl.ds(at, w_b)].reshape(2 * rows, w_b)
        return jnp.dot(rt_ref[...], block, preferred_element_type=jnp.float32)

    phase(step, n_a, 0, ga_ref, w_a, product_a)
    phase(step - n_a, n_b, n_a * w_a, gb_ref, w_b, product_b)


def backward(returned, a, pieces, cols, n_a, n_b):
    rows, width_a = a.shape
    width_b = pieces[0].shape[-1]
    w_a, w_b = width_a // n_a, width_b // n_b
    return pl.pallas_call(
        functools.partial(backward_kernel, ((n_a, w_a), (n_b, w_b))),
        grid=(n_a + n_b,),
        in_specs=[
            pl.BlockSpec((rows // 2, LANES), lambda j: (0, 0)),
            pl.BlockSpec((rows, w_a), lambda j: (0, jnp.minimum(j, n_a - 1))),
        ]
        + [pl.BlockSpec(memory_space=pl.ANY)] * PIECES,
        out_specs=pl.BlockSpec(memory_space=pl.ANY),
        out_shape=jax.ShapeDtypeStruct((cols, 2 * (width_a + width_b)), jnp.bfloat16),
        scratch_shapes=[
            pltpu.VMEM((rows, LANES), jnp.float32),
            pltpu.VMEM((rows, LANES), jnp.float32),
            pltpu.VMEM((2 * cols, rows), jnp.bfloat16),
            pltpu.VMEM((8, 2, 4, 24, width_b), jnp.bfloat16),
            pltpu.VMEM((2, 2 * cols, w_a), jnp.bfloat16),
            pltpu.VMEM((2, 2 * cols, w_b), jnp.bfloat16),
            pltpu.SemaphoreType.DMA((PIECES,)),
            pltpu.SemaphoreType.DMA((2, 2)),
        ],
        cost_estimate=pl.CostEstimate(
            flops=2 * rows * (width_a + width_b) * 2 * cols,
            bytes_accessed=2 * rows * (width_a + width_b) + 4 * cols * (width_a + width_b),
            transcendentals=0,
        ),
    )(returned, a, *pieces)


def gathered(own, width_a):
    xs = lax.axis_size("x")
    a, own_b = own[:, :width_a], own[:, width_a:]
    b = jnp.broadcast_to(own_b[None], (lax.axis_size("z"),) + own_b.shape)
    b = lax.all_to_all(b, "z", split_axis=0, concat_axis=0, tiled=True)
    a = lax.all_gather(a, "x", axis=0, tiled=True)
    a = lax.all_gather(a, ("z", "c"), axis=0, tiled=True)

    def send(v, step):
        return lax.ppermute(v, "x", [(i, (i + step) % xs) for i in range(xs)])

    def swap(v):
        return lax.ppermute(v, "c", [(0, 1), (1, 0)])

    half = b.shape[0] // 2
    fore, back = send(b, 1), send(b, -1)
    mate = swap(b)
    on0, on1 = send(fore[:half], 1), send(back[half:], -1)
    mates = [swap(v) for v in (fore, back, on0, on1)]
    return a, (b, mate, fore, back, on0, on1, *mates)


def local(expert_hidden, probe_tangent, routed_experts, gate_weights):
    tensor = ("z", "x", "c")
    experts = lax.axis_size("expert")
    parts = lax.axis_size(tensor)
    hidden = expert_hidden[0]
    probe = probe_tangent[0]
    cols = probe.shape[0]
    toks = routed_experts.shape[0]
    capacity = hidden.shape[0] * parts // experts

    own = hidden.reshape(2 * hidden.shape[0], hidden.shape[1] // 2)
    width_a = WIDTH_A
    a, pieces = gathered(own, width_a)
    partial = forward_b(pieces, probe, width_a)
    tangent = forward_a(a, probe, partial)
    tangent = lax.all_to_all(
        tangent.reshape(experts, capacity, LANES), "expert", split_axis=0, concat_axis=0, tiled=True
    )
    back, squares = combine(
        tangent.reshape(experts * capacity, LANES), routed_experts.T, gate_weights.T, capacity
    )
    back = lax.all_to_all(
        back.reshape(experts, capacity, LANES),
        "expert",
        split_axis=0,
        concat_axis=0,
        tiled=True,
    )
    shares = lax.all_gather(squares, "x", axis=0, tiled=True)
    shares = jnp.sum(shares, axis=0)
    shares = jnp.broadcast_to(shares[None, None], (lax.axis_size(("z", "c")), 1, toks))
    shares = lax.all_to_all(shares, ("z", "c"), split_axis=0, concat_axis=0, tiled=True)
    gradient = backward(
        back.reshape(experts * capacity, LANES), a, pieces, cols, BLOCKS_A, BLOCKS_B
    )
    quadratic = jnp.sum(shares, axis=(0, 1)) / (cols * parts)
    return gradient[None], quadratic


def solution(mesh):
    grid = Mesh(mesh.devices.reshape(8, 8, 4, 2), ("expert", "z", "x", "c"))
    tensor = ("z", "x", "c")
    return jax.shard_map(
        local,
        mesh=grid,
        in_specs=(
            P("expert", tensor, None),
            P("expert", tensor, None),
            P("expert", None),
            P("expert", None),
        ),
        out_specs=(P("expert", tensor, None), P("expert")),
        check_vma=False,
    )
```
